256 devices in a mesh: region: 32 (over y, z), sub: 8 (over x, core).
Axes of the slice: x: 4, y: 4, z: 8, core: 2. Of those that a mesh axis runs over, the one named last changes fastest.
Arguments:
- mode_rows: bfloat16 [131072, 4096], P(('region', 'sub')), may hold values from -0.09375 to 0.09375
- input_rows: bfloat16 [512, 4096], P(('region', 'sub')), may hold values from -0.25 to 0.25
- input_factor: bfloat16 [512, 128], P(('region', 'sub')), may hold values from -6 to 6
- mode_freq: float32 [4096], replicated, may hold values from 0.5 to 2
- mode_damping: float32 [4096], replicated, may hold values from 0.02 to 0.2
- line_freq: float32 [2], replicated, may hold values from 0.6 to 1.6
- boundary_rows: int32 [32768], P(('region', 'sub')), may hold values from 0 to 511
- connectivity: int32 [4, 131072], P(None, ('region', 'sub')), may hold values from 0 to 639
- stress_coef: float32 [4, 131072], P(None, ('region', 'sub')), may hold values from -3 to 3
Outputs:
- stress_psd: float32 [2, 131072], P(None, ('region', 'sub'))
The draws below stay inside these ranges and needn't reach their ends.
Inputs may be any that keep to these rules, and one draw needn't show every extreme that they name: `boundary_rows`: local row numbers of the sending device. `connectivity`: rows of the node table of the element's device.
All inputs are finite; a program needn't handle non-finite values.
Results may differ from the reference program's by a relative error of at most 0.0013.
Values may be sent and summed in bfloat16 or wider, within the bound.
A program may use at most 64 MiB of HBM per device.

```python
import math
import jax
import jax.numpy as jnp
from jax import lax

M = 4096
NIN = 512
R = 32
LINES = 2
ROWS_DEV = 512
BOUND = 64
ELEM_NODES = 4
ELEM_DEV = 512
DOFS = 131072
ELEMS = 131072
EXPORTS = 32768
DEVICES = 256


def place_ends(array, key, low, top_value):
    place = [jax.random.randint(jax.random.fold_in(key, axis), (), 0, length) for axis, length in enumerate(array.shape)]
    widest = array.shape.index(max(array.shape))
    next_to = place[:widest] + [(place[widest] + 1) % array.shape[widest]] + place[widest + 1:]
    return array.at[tuple(place)].set(low).at[tuple(next_to)].set(top_value)


def block_scale(own_key, dims, pieces, smallest, largest):
    def one(position, blocks):
        draws = jax.random.uniform(jax.random.fold_in(jax.random.fold_in(own_key, 6), position), (blocks,), jnp.float32, smallest / len(pieces), largest / len(pieces))
        return jnp.repeat(jnp.exp(draws), dims[position] // blocks).reshape((-1,) + (1,) * (len(dims) - position - 1))

    level = one(*pieces[0])
    for cut in pieces[1:]:
        level = level * one(*cut)
    return level


def gaussian(own_key, extent, deviation, reach, split=(), dtype=jnp.bfloat16):
    result = deviation * jax.random.normal(own_key, extent, jnp.float32)
    if split:
        result = result * block_scale(own_key, extent, split, -0.22, 0.18)
    return jnp.clip(result, -reach, reach).astype(dtype)


def setup_inputs(seed: int = 0) -> dict:
    streams_of = jax.random.split(jax.random.key(seed), 10)
    return {
        "mode_rows": gaussian(streams_of[0], (DOFS, M), M ** -0.5, 0.09375, ((0, 256),)),
        "input_rows": gaussian(streams_of[1], (NIN, M), NIN ** -0.5, 0.25, ((0, 256),)),
        "input_factor": gaussian(streams_of[2], (NIN, LINES * 2 * R), 1.0, 6.0, ((0, 256),)),
        "mode_freq": jnp.clip(jnp.exp(jax.random.uniform(streams_of[3], (M,), jnp.float32, math.log(0.5), math.log(2.0))), 0.5, 2.0),
        "mode_damping": jnp.clip(jnp.exp(jax.random.uniform(streams_of[4], (M,), jnp.float32, math.log(0.02), math.log(0.2))), 0.02, 0.2),
        "line_freq": jnp.clip(jax.random.uniform(streams_of[5], (LINES,), jnp.float32, 0.6, 1.6), 0.6, 1.6),
        "boundary_rows": place_ends(jax.random.randint(streams_of[6], (EXPORTS,), 0, ROWS_DEV), jax.random.fold_in(streams_of[6], 1), 0, ROWS_DEV - 1).astype(jnp.int32),
        "connectivity": place_ends(jax.random.randint(streams_of[7], (ELEM_NODES, ELEMS), 0, ROWS_DEV + 2 * BOUND), jax.random.fold_in(streams_of[7], 1), 0, (ROWS_DEV + 2 * BOUND) - 1).astype(jnp.int32),
        "stress_coef": gaussian(streams_of[8], (ELEM_NODES, ELEMS), 0.5, 3.0, ((1, 256),), jnp.float32),
    }


def modal_gain(mode_freq, mode_damping, line_omega):
    detune = mode_freq * mode_freq - line_omega * line_omega
    damped = 2.0 * mode_damping * mode_freq * line_omega
    magnitude = detune * detune + damped * damped
    return detune / magnitude, -damped / magnitude


def apply_gain(summed, gain_real, gain_imag):
    half_cols = summed.shape[1] // 2
    forced_real = summed[:, :half_cols]
    forced_imag = summed[:, half_cols:]
    out_real = gain_real[:, None] * forced_real - gain_imag[:, None] * forced_imag
    out_imag = gain_real[:, None] * forced_imag + gain_imag[:, None] * forced_real
    return jnp.concatenate([out_real, out_imag], axis=1).astype(jnp.bfloat16)


def reference(mode_rows, input_rows, input_factor, mode_freq, mode_damping, line_freq, boundary_rows, connectivity, stress_coef):
    line_count = line_freq.shape[0]
    columns = input_factor.shape[1] // line_count
    pseudos = []
    for line_no in range(line_count):
        factor = input_factor[:, line_no * columns:(line_no + 1) * columns]
        summed = lax.dot_general(input_rows, factor, (((0,), (0,)), ((), ())), preferred_element_type=jnp.float32)
        gain_real, gain_imag = modal_gain(mode_freq, mode_damping, line_freq[line_no])
        pseudos.append(apply_gain(summed, gain_real, gain_imag))

    def recover(shapes_block):
        parts_list = [jnp.dot(shapes_block, pseudo, preferred_element_type=jnp.float32).astype(jnp.bfloat16) for pseudo in pseudos]
        return jnp.concatenate(parts_list, axis=1)

    responses = lax.map(recover, mode_rows.reshape(DEVICES, ROWS_DEV, M))
    width_all = responses.shape[2]
    picks = boundary_rows.reshape(DEVICES, 2 * BOUND)
    exports = jax.vmap(lambda node_rows, chosen: node_rows[chosen])(responses, picks)
    blank = jnp.zeros((1, BOUND, width_all), jnp.bfloat16)
    lower = jnp.concatenate([blank, exports[:-1, BOUND:]], axis=0)
    upper = jnp.concatenate([exports[1:, :BOUND], blank], axis=0)
    node_table = jnp.concatenate([lower, responses, upper], axis=1)
    links = connectivity.reshape(ELEM_NODES, DEVICES, ELEM_DEV).transpose(1, 0, 2)
    weights = stress_coef.reshape(ELEM_NODES, DEVICES, ELEM_DEV).transpose(1, 0, 2)
    gathered = jax.vmap(lambda node_rows, chosen: node_rows[chosen])(node_table, links)
    stress = jnp.sum(weights[:, :, :, None] * gathered.astype(jnp.float32), axis=1)
    squares = (stress * stress).reshape(DEVICES, ELEM_DEV, line_count, columns)
    power = jnp.mean(squares, axis=3)
    return power.transpose(2, 0, 1).reshape(line_count, DEVICES * ELEM_DEV)
```

```python
import jax
import jax.numpy as jnp
from jax import lax
from jax.experimental import pallas as pl
from jax.experimental.pallas import tpu as pltpu
from jax.sharding import PartitionSpec as P

MESH = pl.DeviceIdType.MESH
NY, NZ, NX, NC = 4, 8, 4, 2
NPLANE = NY * NX * NC
DEVICES = NPLANE * NZ
LINES = 2
R = 32
BOUND = 64
F32 = jnp.float32
BF16 = jnp.bfloat16


def kernel(
    mode_hbm, rows_hbm, factor_hbm, freq_hbm, damp_hbm, line_hbm, brow_hbm, conn_hbm, coef_hbm,
    out_ref,
    modes, rows_v, factor_v, freq_v, damp_v, line_s, brow_v, conn_v, coef_v,
    r1, f1, r2, f2, pbuf, export, w_hi, w_lo, acc,
    load_sem, s1_send, s1_rrecv, s1_frecv, s2_send, s2_rrecv, s2_frecv,
    s3_send, s3_recv, s3_core, e_send, e_recv, own_sem,
):
    region = lax.axis_index("region")
    sub = lax.axis_index("sub")
    y, z = region // NZ, region % NZ
    x, c = sub // NC, sub % NC
    dev = region * (NX * NC) + sub
    q = (y * NX + x) * NC + c
    own = mode_hbm.shape[0]
    nodes = own + 2 * BOUND

    def device(yy, zz, xx, cc):
        return {"region": yy * NZ + zz, "sub": xx * NC + cc}

    plane = [(i, j, k) for i in range(NY) for j in range(NX) for k in range(NC)]
    plane = sorted(plane[1:], key=lambda o: -(min(o[0], NY - o[0]) + min(o[1], NX - o[1])))
    zs = [4, 3, 5, 2, 6, 1, 7]

    def plane_peer(o):
        yy, xx, cc = (y + o[0]) % NY, (x + o[1]) % NX, (c + o[2]) % NC
        return device(yy, z, xx, cc), (yy * NX + xx) * NC + cc

    nxt = (dev + 1) % DEVICES
    prv = (dev + DEVICES - 1) % DEVICES
    next_dev = {"region": nxt // (NX * NC), "sub": nxt % (NX * NC)}
    prev_dev = {"region": prv // (NX * NC), "sub": prv % (NX * NC)}

    loads = [
        pltpu.make_async_copy(rows_hbm, rows_v, load_sem.at[0]),
        pltpu.make_async_copy(factor_hbm, factor_v, load_sem.at[1]),
        pltpu.make_async_copy(conn_hbm, conn_v, load_sem.at[2]),
        pltpu.make_async_copy(coef_hbm, coef_v, load_sem.at[3]),
        pltpu.make_async_copy(mode_hbm, modes.at[pl.ds(BOUND, own)], load_sem.at[4]),
        pltpu.make_async_copy(brow_hbm, brow_v, load_sem.at[5]),
        pltpu.make_async_copy(freq_hbm, freq_v, load_sem.at[6]),
        pltpu.make_async_copy(damp_hbm, damp_v, load_sem.at[7]),
        pltpu.make_async_copy(line_hbm, line_s, load_sem.at[8]),
    ]
    for copy in loads:
        copy.start()

    barrier = pltpu.get_barrier_semaphore()
    greet = [plane_peer(o)[0] for o in plane]
    greet += [device(y, (z + k) % NZ, x, c) for k in zs]
    greet += [next_dev, prev_dev]
    for peer in greet:
        pl.semaphore_signal(barrier, inc=1, device_id=peer, device_id_type=MESH)

    for copy in loads[:4]:
        copy.wait()

    block = 64

    def build(step, carry):
        base = pl.multiple_of(step * block, block)
        node = base + lax.broadcasted_iota(jnp.int32, (block, conn_v.shape[1]), 0)
        total = jnp.zeros((block, conn_v.shape[1]), F32)
        for k in range(conn_v.shape[0]):
            total = total + jnp.where(node == conn_v[k : k + 1, :], coef_v[k : k + 1, :], 0.0)
        high = total.astype(BF16)
        w_hi[pl.ds(base, block), :] = high
        w_lo[pl.ds(base, block), :] = (total - high.astype(F32)).astype(BF16)
        return carry

    lax.fori_loop(0, nodes // block, build, 0)

    pl.semaphore_wait(barrier, len(greet))

    def remote(src, dst, send, recv, peer):
        return pltpu.make_async_remote_copy(
            src_ref=src, dst_ref=dst, send_sem=send, recv_sem=recv, device_id=peer, device_id_type=MESH
        )

    my_pair = r1.at[pl.ds(2 * q, 2)]
    for o in plane:
        peer, chunk = plane_peer(o)
        src = rows_v.at[:, pl.ds(pl.multiple_of(chunk * 128, 128), 128)]
        remote(src, my_pair, s1_send.at[0], s1_rrecv, peer).start()
    for k in zs:
        remote(factor_v, f1.at[z], s1_send.at[1], s1_frecv, device(y, (z + k) % NZ, x, c)).start()
    own_rows = pltpu.make_async_copy(
        rows_v.at[:, pl.ds(pl.multiple_of(q * 128, 128), 128)], my_pair, own_sem.at[0]
    )
    own_factor = pltpu.make_async_copy(factor_v, f1.at[z], own_sem.at[1])
    own_rows.start()
    own_factor.start()

    for copy in loads[4:]:
        copy.wait()
    picks = lax.broadcasted_iota(jnp.int32, (own, 2 * BOUND), 0) == brow_v[...]
    picks = jnp.where(picks, 1.0, 0.0).T.astype(BF16)
    width = 512

    def pick(step, carry):
        cols = pl.ds(pl.multiple_of(step * width, width), width)
        export[:, cols] = jnp.dot(
            picks, modes[pl.ds(BOUND, own), cols], preferred_element_type=F32
        ).astype(BF16)
        return carry

    lax.fori_loop(0, modes.shape[1] // width, pick, 0)

    own_rows.wait()
    own_factor.wait()
    got = r1.at[pl.ds(0, 2 * (NPLANE - 1))]
    pltpu.make_async_copy(got, got, s1_rrecv).wait()
    got = f1.at[pl.ds(0, NZ - 1)]
    pltpu.make_async_copy(got, got, s1_frecv).wait()

    for k in zs:
        remote(r1, r2.at[z], s2_send.at[0], s2_rrecv, device(y, (z + k) % NZ, x, c)).start()
    for o in plane:
        remote(f1, f2.at[:, q], s2_send.at[1], s2_frecv, plane_peer(o)[0]).start()
    own_rows = pltpu.make_async_copy(r1, r2.at[z], own_sem.at[0])
    own_factor = pltpu.make_async_copy(f1, f2.at[:, q], own_sem.at[1])
    own_rows.start()
    own_factor.start()

    to_prev = remote(
        export.at[pl.ds(0, BOUND)], modes.at[pl.ds(own + BOUND, BOUND)], e_send.at[0], e_recv.at[0], prev_dev
    )
    to_next = remote(
        export.at[pl.ds(BOUND, BOUND)], modes.at[pl.ds(0, BOUND)], e_send.at[1], e_recv.at[1], next_dev
    )
    to_prev.start()
    to_next.start()

    freq = freq_v[pl.ds(q, 1), :]
    damp = damp_v[pl.ds(q, 1), :]
    gains = []
    for line in range(LINES):
        omega = line_s[line]
        detune = freq * freq - omega * omega
        damped = 2.0 * damp * freq * omega
        magnitude = detune * detune + damped * damped
        gains.append((detune / magnitude, -damped / magnitude))

    own_rows.wait()
    own_factor.wait()
    got = r2.at[pl.ds(0, NZ - 1)]
    pltpu.make_async_copy(got, got, s2_rrecv).wait()
    got = f2.at[:, pl.ds(0, NPLANE - 1)]
    pltpu.make_async_copy(got, got, s2_frecv).wait()

    inputs = NZ * NPLANE * 2
    forced = lax.dot_general(
        f2.reshape(inputs, 128)[...], r2.reshape(inputs, 128)[...],
        (((0,), (0,)), ((), ())), preferred_element_type=F32,
    )
    parts = []
    for line in range(LINES):
        real = forced[line * 2 * R : line * 2 * R + R]
        imag = forced[line * 2 * R + R : (line + 1) * 2 * R]
        gain_real, gain_imag = gains[line]
        parts.append(gain_real * real - gain_imag * imag)
        parts.append(gain_real * imag + gain_imag * real)
    pbuf[pl.ds(pl.multiple_of(q * 128, 128), 128), :] = jnp.concatenate(parts, axis=0).T.astype(BF16)

    grid = [(i, j) for i in range(NY) for j in range(NX)]
    near = sorted(grid, key=lambda o: min(o[0], NY - o[0]) + min(o[1], NX - o[1]))
    core_peer = device(y, z, x, 1 - c)

    def chunk_rows(pair, core):
        return pl.ds(pl.multiple_of((pair * NC + core) * 128, 128), 128)

    mine = pbuf.at[chunk_rows(y * NX + x, c)]
    for i, j in reversed(near[1:]):
        peer = device((y + i) % NY, z, (x + j) % NX, c)
        remote(mine, mine, s3_send, s3_recv.at[i * NX + j], peer).start()

    def source(o):
        return ((y + NY - o[0]) % NY) * NX + (x + NX - o[1]) % NX

    def add(o, first):
        pair = source(o)
        landed = pbuf.at[chunk_rows(pair, 1 - c)]
        pltpu.make_async_copy(landed, landed, s3_core.at[o[0] * NX + o[1]]).wait()
        span = pl.ds(pl.multiple_of(pair * 256, 256), 256)
        term = jnp.dot(modes[:, span], pbuf[span, :], preferred_element_type=F32)
        acc[...] = term if first else acc[...] + term

    before = None
    for n, o in enumerate(near):
        piece = pbuf.at[chunk_rows(source(o), c)]
        if n:
            pltpu.make_async_copy(piece, piece, s3_recv.at[o[0] * NX + o[1]]).wait()
        remote(piece, piece, s3_send, s3_core.at[o[0] * NX + o[1]], core_peer).start()
        if n == 0:
            to_prev.wait_recv()
            to_next.wait_recv()
        if before is not None:
            add(before, n == 1)
        before = o
    add(before, False)

    responses = acc[...]
    lower = jnp.where(dev > 0, responses[:BOUND], 0.0)
    upper = jnp.where(dev < DEVICES - 1, responses[own + BOUND :], 0.0)
    table = jnp.concatenate([lower, responses[BOUND : own + BOUND], upper], axis=0)
    table = table.T.astype(BF16)
    stress = jnp.dot(table, w_hi[...], preferred_element_type=F32)
    stress = stress + jnp.dot(table, w_lo[...], preferred_element_type=F32)
    squares = stress * stress
    for line in range(LINES):
        part = squares[line * 2 * R : (line + 1) * 2 * R]
        out_ref[line : line + 1, :] = jnp.sum(part, axis=0, keepdims=True) * (1.0 / (2 * R))

    got = r1.at[pl.ds(0, 2 * (NPLANE - 1))]
    pltpu.make_async_copy(got, got, s1_send.at[0]).wait()
    got = f1.at[pl.ds(0, NZ - 1)]
    pltpu.make_async_copy(got, got, s1_send.at[1]).wait()
    got = r2.at[pl.ds(0, NZ - 1)]
    pltpu.make_async_copy(got, got, s2_send.at[0]).wait()
    got = f2.at[:, pl.ds(0, NPLANE - 1)]
    pltpu.make_async_copy(got, got, s2_send.at[1]).wait()
    got = pbuf.at[pl.ds(0, 128 * (2 * NY * NX - 1))]
    pltpu.make_async_copy(got, got, s3_send).wait()
    to_prev.wait_send()
    to_next.wait_send()


def local(
    mode_rows, input_rows, input_factor, mode_freq, mode_damping, line_freq, boundary_rows, connectivity,
    stress_coef,
):
    own, modes = mode_rows.shape
    nodes = own + 2 * BOUND
    elements = connectivity.shape[1]
    dma = pltpu.SemaphoreType.DMA
    return pl.pallas_call(
        kernel,
        name="modal_stress",
        out_shape=jax.ShapeDtypeStruct((LINES, elements), F32),
        in_specs=[pl.BlockSpec(memory_space=pl.ANY)] * 9,
        out_specs=pl.BlockSpec(memory_space=pltpu.VMEM),
        scratch_shapes=[
            pltpu.VMEM((nodes, modes), BF16),
            pltpu.VMEM((2, modes), BF16),
            pltpu.VMEM((2, 128), BF16),
            pltpu.VMEM((NPLANE, 128), F32),
            pltpu.VMEM((NPLANE, 128), F32),
            pltpu.SMEM((LINES,), F32),
            pltpu.VMEM((1, 2 * BOUND), jnp.int32),
            pltpu.VMEM(connectivity.shape, jnp.int32),
            pltpu.VMEM(stress_coef.shape, F32),
            pltpu.VMEM((2 * NPLANE, 128), BF16),
            pltpu.VMEM((NZ, 2, 128), BF16),
            pltpu.VMEM((NZ, 2 * NPLANE, 128), BF16),
            pltpu.VMEM((NZ, NPLANE, 2, 128), BF16),
            pltpu.VMEM((modes, 128), BF16),
            pltpu.VMEM((2 * BOUND, modes), BF16),
            pltpu.VMEM((nodes, elements), BF16),
            pltpu.VMEM((nodes, elements), BF16),
            pltpu.VMEM((nodes, 128), F32),
            dma((9,)),
            dma((2,)),
            dma(()),
            dma(()),
            dma((2,)),
            dma(()),
            dma(()),
            dma(()),
            dma((NY * NX,)),
            dma((NY * NX,)),
            dma((2,)),
            dma((2,)),
            dma((2,)),
        ],
        compiler_params=pltpu.CompilerParams(
            collective_id=0, has_side_effects=True, vmem_limit_bytes=48 << 20
        ),
    )(
        mode_rows,
        input_rows,
        input_factor,
        mode_freq.reshape(NPLANE, 128),
        mode_damping.reshape(NPLANE, 128),
        line_freq,
        boundary_rows.reshape(1, 2 * BOUND),
        connectivity,
        stress_coef,
    )


def solution(mesh):
    split = ("region", "sub")
    placed = (
        P(split, None),
        P(split, None),
        P(split, None),
        P(),
        P(),
        P(),
        P(split),
        P(None, split),
        P(None, split),
    )
    return jax.shard_map(
        local, mesh=mesh, in_specs=placed, out_specs=P(None, split), check_vma=False
    )
```

```python
import jax
import jax.numpy as jnp
from jax import lax
from jax.experimental import pallas as pl
from jax.experimental.pallas import tpu as pltpu
from jax.sharding import PartitionSpec as P

MESH = pl.DeviceIdType.MESH
NY, NZ, NX, NC = 4, 8, 4, 2
NPLANE = NY * NX * NC
DEVICES = NPLANE * NZ
LINES = 2
R = 32
BOUND = 64
LAG = 3
F32 = jnp.float32
BF16 = jnp.bfloat16


def kernel(
    mode_hbm, rows_hbm, factor_hbm, freq_hbm, damp_hbm, line_hbm, brow_hbm, conn_hbm, coef_hbm,
    out_ref,
    modes, rows_v, factor_v, freq_v, damp_v, line_s, brow_v, conn_v, coef_v,
    r1, f1, r2, f2, pbuf, export, w_hi, w_lo, acc,
    load_sem, s1_send, s1_rrecv, s1_frecv, s2_send, s2_rrecv, s2_frecv,
    s3_send, s3_recv, s3_core, e_send, e_recv, own_sem,
):
    region = lax.axis_index("region")
    sub = lax.axis_index("sub")
    y, z = region // NZ, region % NZ
    x, c = sub // NC, sub % NC
    dev = region * (NX * NC) + sub
    q = (c * NY + y) * NX + x
    own = mode_hbm.shape[0]
    nodes = own + 2 * BOUND

    def device(yy, zz, xx, cc):
        return {"region": yy * NZ + zz, "sub": xx * NC + cc}

    plane = [(i, j, k) for i in range(NY) for j in range(NX) for k in range(NC)]
    plane = sorted(plane[1:], key=lambda o: -(min(o[0], NY - o[0]) + min(o[1], NX - o[1])))
    zs = [4, 3, 5, 2, 6, 1, 7]

    def plane_peer(o):
        yy, xx, cc = (y + o[0]) % NY, (x + o[1]) % NX, (c + o[2]) % NC
        return device(yy, z, xx, cc), (cc * NY + yy) * NX + xx

    nxt = (dev + 1) % DEVICES
    prv = (dev + DEVICES - 1) % DEVICES
    next_dev = {"region": nxt // (NX * NC), "sub": nxt % (NX * NC)}
    prev_dev = {"region": prv // (NX * NC), "sub": prv % (NX * NC)}

    loads = [
        pltpu.make_async_copy(mode_hbm, modes.at[pl.ds(BOUND, own)], load_sem.at[4]),
        pltpu.make_async_copy(brow_hbm, brow_v, load_sem.at[5]),
        pltpu.make_async_copy(rows_hbm, rows_v, load_sem.at[0]),
        pltpu.make_async_copy(factor_hbm, factor_v, load_sem.at[1]),
        pltpu.make_async_copy(conn_hbm, conn_v, load_sem.at[2]),
        pltpu.make_async_copy(coef_hbm, coef_v, load_sem.at[3]),
        pltpu.make_async_copy(freq_hbm, freq_v, load_sem.at[6]),
        pltpu.make_async_copy(damp_hbm, damp_v, load_sem.at[7]),
        pltpu.make_async_copy(line_hbm, line_s, load_sem.at[8]),
    ]
    for copy in loads:
        copy.start()

    barrier = pltpu.get_barrier_semaphore()
    greet = [device(y, (z + k) % NZ, x, c) for k in zs[:3]]
    greet += [plane_peer(o)[0] for o in plane[:8]]
    greet += [next_dev, prev_dev]
    greet += [device(y, (z + k) % NZ, x, c) for k in zs[3:]]
    greet += [plane_peer(o)[0] for o in plane[8:]]
    for peer in greet:
        pl.semaphore_signal(barrier, inc=1, device_id=peer, device_id_type=MESH)

    for copy in loads[:4]:
        copy.wait()
    picks = lax.broadcasted_iota(jnp.int32, (own, 2 * BOUND), 0) == brow_v[...]
    picks = jnp.where(picks, 1.0, 0.0).T.astype(BF16)
    width = 512

    def pick(step, carry):
        cols = pl.ds(pl.multiple_of(step * width, width), width)
        export[:, cols] = jnp.dot(
            picks, modes[pl.ds(BOUND, own), cols], preferred_element_type=F32
        ).astype(BF16)
        return carry

    lax.fori_loop(0, modes.shape[1] // width, pick, 0)

    pl.semaphore_wait(barrier, len(greet))

    def remote(src, dst, send, recv, peer):
        return pltpu.make_async_remote_copy(
            src_ref=src, dst_ref=dst, send_sem=send, recv_sem=recv, device_id=peer, device_id_type=MESH
        )

    pending = []

    def drain(part, sem):
        pending.append(pltpu.make_async_copy(part, part, sem).wait)

    for k in zs:
        remote(factor_v, f1.at[z], s1_send.at[1], s1_frecv, device(y, (z + k) % NZ, x, c)).start()
    my_pair = r1.at[pl.ds(2 * q, 2)]
    for o in plane:
        peer, chunk = plane_peer(o)
        src = rows_v.at[:, pl.ds(pl.multiple_of(chunk * 128, 128), 128)]
        remote(src, my_pair, s1_send.at[0], s1_rrecv, peer).start()
    own_rows = pltpu.make_async_copy(
        rows_v.at[:, pl.ds(pl.multiple_of(q * 128, 128), 128)], my_pair, own_sem.at[0]
    )
    own_factor = pltpu.make_async_copy(factor_v, f1.at[z], own_sem.at[1])
    own_rows.start()
    own_factor.start()
    drain(r1.at[pl.ds(0, 2 * (NPLANE - 1))], s1_send.at[0])
    drain(f1.at[pl.ds(0, NZ - 1)], s1_send.at[1])

    to_prev = remote(
        export.at[pl.ds(0, BOUND)], modes.at[pl.ds(own + BOUND, BOUND)], e_send.at[0], e_recv.at[0], prev_dev
    )
    to_next = remote(
        export.at[pl.ds(BOUND, BOUND)], modes.at[pl.ds(0, BOUND)], e_send.at[1], e_recv.at[1], next_dev
    )
    to_prev.start()
    to_next.start()
    pending.append(to_prev.wait_send)
    pending.append(to_next.wait_send)

    for copy in loads[4:]:
        copy.wait()

    block = 64

    def build(step, carry):
        base = pl.multiple_of(step * block, block)
        node = base + lax.broadcasted_iota(jnp.int32, (block, conn_v.shape[1]), 0)
        total = jnp.zeros((block, conn_v.shape[1]), F32)
        for k in range(conn_v.shape[0]):
            total = total + jnp.where(node == conn_v[k : k + 1, :], coef_v[k : k + 1, :], 0.0)
        high = total.astype(BF16)
        w_hi[pl.ds(base, block), :] = high
        w_lo[pl.ds(base, block), :] = (total - high.astype(F32)).astype(BF16)
        return carry

    lax.fori_loop(0, nodes // block, build, 0)

    own_factor.wait()
    got = f1.at[pl.ds(0, NZ - 1)]
    pltpu.make_async_copy(got, got, s1_frecv).wait()
    for o in plane:
        remote(f1, f2.at[:, q], s2_send.at[1], s2_frecv, plane_peer(o)[0]).start()
    own_factor = pltpu.make_async_copy(f1, f2.at[:, q], own_sem.at[1])
    own_factor.start()
    drain(f2.at[:, pl.ds(0, NPLANE - 1)], s2_send.at[1])

    own_rows.wait()
    got = r1.at[pl.ds(0, 2 * (NPLANE - 1))]
    pltpu.make_async_copy(got, got, s1_rrecv).wait()
    for k in zs:
        remote(r1, r2.at[z], s2_send.at[0], s2_rrecv, device(y, (z + k) % NZ, x, c)).start()
    own_rows = pltpu.make_async_copy(r1, r2.at[z], own_sem.at[0])
    own_rows.start()
    drain(r2.at[pl.ds(0, NZ - 1)], s2_send.at[0])

    freq = freq_v[pl.ds(q, 1), :]
    damp = damp_v[pl.ds(q, 1), :]
    gains = []
    for line in range(LINES):
        omega = line_s[line]
        detune = freq * freq - omega * omega
        damped = 2.0 * damp * freq * omega
        magnitude = detune * detune + damped * damped
        gains.append((detune / magnitude, -damped / magnitude))

    own_rows.wait()
    own_factor.wait()
    got = r2.at[pl.ds(0, NZ - 1)]
    pltpu.make_async_copy(got, got, s2_rrecv).wait()
    got = f2.at[:, pl.ds(0, NPLANE - 1)]
    pltpu.make_async_copy(got, got, s2_frecv).wait()

    inputs = NZ * NPLANE * 2
    forced = lax.dot_general(
        f2.reshape(inputs, 128)[...], r2.reshape(inputs, 128)[...],
        (((0,), (0,)), ((), ())), preferred_element_type=F32,
    )
    parts = []
    for line in range(LINES):
        real = forced[line * 2 * R : line * 2 * R + R]
        imag = forced[line * 2 * R + R : (line + 1) * 2 * R]
        gain_real, gain_imag = gains[line]
        parts.append(gain_real * real - gain_imag * imag)
        parts.append(gain_real * imag + gain_imag * real)
    pbuf[pl.ds(pl.multiple_of(q * 128, 128), 128), :] = jnp.concatenate(parts, axis=0).T.astype(BF16)

    def flip(v, bits):
        return (v, v + 1 - 2 * (v % 2), (v + 2) % 4, 3 - v)[bits]

    hops = (0, 1, 2, 1)
    offsets = [(i, j) for i in range(NY) for j in range(NX)]
    mine = pbuf.at[pl.ds(pl.multiple_of(q * 128, 128), 128)]
    for i, j in sorted(offsets[1:], key=lambda o: -hops[o[0]] - hops[o[1]]):
        peer = device(flip(y, i), z, flip(x, j), c)
        remote(mine, mine, s3_send, s3_recv.at[i * NX + j], peer).start()

    core_peer = device(y, z, x, 1 - c)
    pairs = [(i, h) for i in range(NY) for h in range(2)]
    pairs = sorted(pairs, key=lambda p: hops[p[0]] + p[1])

    def span(pair, core):
        i, h = pair
        half = x // 2 if h == 0 else 1 - x // 2
        return pl.ds(pl.multiple_of(((core * NY + flip(y, i)) * NX + 2 * half) * 128, 256), 256)

    def add(rows, first=False):
        term = jnp.dot(modes[:, rows], pbuf[rows, :], preferred_element_type=F32)
        acc[...] = term if first else acc[...] + term

    def add_other(pair):
        rows = span(pair, 1 - c)
        landed = pbuf.at[rows]
        pltpu.make_async_copy(landed, landed, s3_core.at[pair[0] * 2 + pair[1]]).wait()
        add(rows)

    for n, pair in enumerate(pairs):
        rows = span(pair, c)
        piece = pbuf.at[rows]
        for j in (2 * pair[1], 2 * pair[1] + 1):
            if (pair[0], j) != (0, 0):
                pltpu.make_async_copy(mine, mine, s3_recv.at[pair[0] * NX + j]).wait()
        remote(piece, piece, s3_send, s3_core.at[pair[0] * 2 + pair[1]], core_peer).start()
        if n == 0:
            to_prev.wait_recv()
            to_next.wait_recv()
        add(rows, n == 0)
        if n >= LAG:
            add_other(pairs[n - LAG])
    for pair in pairs[len(pairs) - LAG :]:
        add_other(pair)

    responses = acc[...]
    lower = jnp.where(dev > 0, responses[:BOUND], 0.0)
    upper = jnp.where(dev < DEVICES - 1, responses[own + BOUND :], 0.0)
    table = jnp.concatenate([lower, responses[BOUND : own + BOUND], upper], axis=0)
    table = table.T.astype(BF16)
    stress = jnp.dot(table, w_hi[...], preferred_element_type=F32)
    stress = stress + jnp.dot(table, w_lo[...], preferred_element_type=F32)
    squares = stress * stress
    for line in range(LINES):
        part = squares[line * 2 * R : (line + 1) * 2 * R]
        out_ref[line : line + 1, :] = jnp.sum(part, axis=0, keepdims=True) * (1.0 / (2 * R))

    drain(pbuf.at[pl.ds(0, 128 * (2 * NY * NX - 1))], s3_send)
    for wait in pending:
        wait()


def local(
    mode_rows, input_rows, input_factor, mode_freq, mode_damping, line_freq, boundary_rows, connectivity,
    stress_coef,
):
    own, modes = mode_rows.shape
    nodes = own + 2 * BOUND
    elements = connectivity.shape[1]
    dma = pltpu.SemaphoreType.DMA
    return pl.pallas_call(
        kernel,
        name="modal_stress",
        out_shape=jax.ShapeDtypeStruct((LINES, elements), F32),
        in_specs=[pl.BlockSpec(memory_space=pl.ANY)] * 9,
        out_specs=pl.BlockSpec(memory_space=pltpu.VMEM),
        scratch_shapes=[
            pltpu.VMEM((nodes, modes), BF16),
            pltpu.VMEM((2, modes), BF16),
            pltpu.VMEM((2, 128), BF16),
            pltpu.VMEM((NPLANE, 128), F32),
            pltpu.VMEM((NPLANE, 128), F32),
            pltpu.SMEM((LINES,), F32),
            pltpu.VMEM((1, 2 * BOUND), jnp.int32),
            pltpu.VMEM(connectivity.shape, jnp.int32),
            pltpu.VMEM(stress_coef.shape, F32),
            pltpu.VMEM((2 * NPLANE, 128), BF16),
            pltpu.VMEM((NZ, 2, 128), BF16),
            pltpu.VMEM((NZ, 2 * NPLANE, 128), BF16),
            pltpu.VMEM((NZ, NPLANE, 2, 128), BF16),
            pltpu.VMEM((modes, 128), BF16),
            pltpu.VMEM((2 * BOUND, modes), BF16),
            pltpu.VMEM((nodes, elements), BF16),
            pltpu.VMEM((nodes, elements), BF16),
            pltpu.VMEM((nodes, 128), F32),
            dma((9,)),
            dma((2,)),
            dma(()),
            dma(()),
            dma((2,)),
            dma(()),
            dma(()),
            dma(()),
            dma((NY * NX,)),
            dma((NY * 2,)),
            dma((2,)),
            dma((2,)),
            dma((2,)),
        ],
        compiler_params=pltpu.CompilerParams(
            collective_id=0, has_side_effects=True, vmem_limit_bytes=62 << 20
        ),
    )(
        mode_rows,
        input_rows,
        input_factor,
        mode_freq.reshape(NPLANE, 128),
        mode_damping.reshape(NPLANE, 128),
        line_freq,
        boundary_rows.reshape(1, 2 * BOUND),
        connectivity,
        stress_coef,
    )


def solution(mesh):
    split = ("region", "sub")
    placed = (
        P(split, None),
        P(split, None),
        P(split, None),
        P(),
        P(),
        P(),
        P(split),
        P(None, split),
        P(None, split),
    )
    return jax.shard_map(
        local, mesh=mesh, in_specs=placed, out_specs=P(None, split), check_vma=False
    )
```
